32 devices in a mesh: vocab: 8 (over z, x), width: 4 (over y, core).
Axes of the slice: x: 2, y: 2, z: 4, core: 2. Of those that a mesh axis runs over, the one named last changes fastest.
Arguments:
- hidden: bfloat16 [384, 2048], P('vocab', 'width'), may hold values from -2000 to 2000, as said below
- norm_gain: bfloat16 [2048], replicated, may hold values from 0.25 to 1.75
- head_weight: bfloat16 [2048, 163840], P('width', 'vocab'), may hold values from -8 to 8, as said below
- lengths: int32 [16], replicated, may hold values from 1 to 96, 384 in all
- deal: int32 [384], P('width'), may hold values from 0 to 383, each once
- targets: int32 [384], P('width'), may hold values from 0 to 163839
Outputs:
- token_logprob: float32 [384], P('vocab')
- request_stats: float32 [4, 16], replicated
The draws below stay inside these ranges and needn't reach their ends.
Inputs may be any that keep to these rules, and one draw needn't show every extreme that they name: The 16 lengths sum to 384. `deal`: each position occurs once. `hidden`: real values. `head_weight`: real values.
All inputs are finite; a program needn't handle non-finite values.
Results may differ from the reference program's by a relative error of at most 0.00055.
Values may be sent and summed in bfloat16 or wider, within the bound.
A program may use at most 128 MiB of HBM per device.

```python
import math
import jax
import jax.numpy as jnp
import numpy as np
from jax import lax

D = 2048
VOCAB = 163840
REQS = 16
TOKENS = 384


def draw_head_weight(key, part):
    scale = 3.0 / math.sqrt(D)
    base = jnp.clip(jax.random.normal(jax.random.fold_in(key, 1), (D, VOCAB), jnp.float32), -6.0, 6.0) * scale
    return base.astype(jnp.bfloat16)


def draw_hidden(key, part):
    spread = jax.random.uniform(jax.random.fold_in(key, 3), (D,), jnp.float32)
    position = jnp.arange(D, dtype=jnp.float32) / D
    col_scale = jnp.exp(math.log(10.0) * (0.5 * position + 0.5 * spread))
    rising = jax.random.uniform(jax.random.fold_in(key, 4), (TOKENS, 1), jnp.float32)
    row_scale = jnp.exp(math.log(10.0) * rising)
    noise = jnp.clip(jax.random.normal(jax.random.fold_in(key, 5), (TOKENS, D), jnp.float32), -5.0, 5.0)
    base = noise * col_scale[None, :] * row_scale
    return base.astype(jnp.bfloat16)


def set_ends(result, rng, low, high):
    shape = result.shape
    spot = [jax.random.randint(jax.random.fold_in(rng, axis), (), 0, shape[axis]) for axis in range(len(shape))]
    result = result.at[tuple(spot)].set(low)
    longest = shape.index(max(shape))
    spot[longest] = (spot[longest] + 1) % shape[longest]
    return result.at[tuple(spot)].set(high)


def ranked_wide(rng, extent, count, skew):
    loads = [min(1 << octave, count + 1 - (1 << octave)) * (1 << 20) // math.isqrt((1 << octave) ** skew) + 1 for octave in range((count + 1).bit_length()) if 1 << octave <= count]
    scale = 1 + sum(loads) // (1 << 30)
    listing = np.cumsum(np.array([max(1, weight // scale) for weight in loads]))
    lot = jax.random.randint(jax.random.fold_in(rng, 1), extent, 0, int(listing[len(loads) - 1]))
    start = jnp.left_shift(1, jnp.searchsorted(jnp.asarray(listing, jnp.int32), lot, side="right").astype(jnp.int32))
    rank = start - 1 + jax.random.randint(jax.random.fold_in(rng, 4), extent, 0, 1 << 30) % jnp.minimum(start, count + 1 - start)
    return jax.random.permutation(jax.random.fold_in(rng, 2), count)[rank].astype(jnp.int32)


def split_up(number_of, total, reach, slope):
    loads = [(1 << 20) // math.isqrt(standing ** slope) + 1 for standing in range(2, number_of + 1)]
    surplus, given = total - reach - (number_of - 1), [1] * (number_of - 1)
    while surplus > 0:
        free = [i for i in range(number_of - 1) if given[i] < reach]
        pool, left = sum([loads[i] for i in free]), surplus
        for i in free:
            addition = min(reach - given[i], max(1, left * loads[i] // pool), surplus)
            given[i] = given[i] + addition
            surplus = surplus - addition
    return np.array([reach] + given)


def uneven(rng, count, total, most, slope):
    if count == 2:
        one = jax.random.randint(rng, (), max(1, total - most), min(most, total - 1) + 1)
        return jnp.stack([one, total - one])
    sizes = jnp.asarray(split_up(count, total, most, slope), jnp.int32)
    twos = (count - 1) // 2
    donor, receiver = sizes[1:1 + 2 * twos:2], sizes[2:2 + 2 * twos:2]
    margin = jnp.minimum(donor - 1, most - receiver)
    moved = jax.random.randint(jax.random.fold_in(rng, 1), (twos,), 0, 1 << 20) % (margin + 1)
    sizes = sizes.at[1:1 + 2 * twos:2].set(donor - moved).at[2:2 + 2 * twos:2].set(receiver + moved)
    return sizes[jax.random.permutation(jax.random.fold_in(rng, 2), count)]


def setup_inputs(seed: int = 0) -> dict:
    streams_of = jax.random.split(jax.random.key(seed), 7)
    return {
        "hidden": draw_hidden(jax.random.fold_in(streams_of[6], 71), 0),
        "norm_gain": jnp.clip(1.0 + 0.15 * jax.random.normal(streams_of[1], (D,), jnp.float32), 0.25, 1.75).astype(jnp.bfloat16),
        "head_weight": draw_head_weight(jax.random.fold_in(streams_of[6], 71), 0),
        "lengths": uneven(streams_of[3], REQS, TOKENS, TOKENS // 4, 2).astype(jnp.int32),
        "deal": jax.random.permutation(streams_of[4], TOKENS).astype(jnp.int32),
        "targets": set_ends(ranked_wide(streams_of[5], (TOKENS,), VOCAB, 2), jax.random.fold_in(streams_of[5], 3), 0, VOCAB - 1).astype(jnp.int32),
    }


epsilon = 1e-06

def reference(hidden, norm_gain, head_weight, lengths, deal, targets):
    tokens = hidden.shape[0]
    widened = hidden.astype(jnp.float32)
    mean_sq = lax.optimization_barrier(jnp.mean(widened * widened, axis=1))
    normed = (widened * lax.rsqrt(mean_sq + epsilon)[:, None] * norm_gain[None, :]).astype(jnp.bfloat16)
    block = math.gcd(tokens, 512)
    columns = lax.iota(jnp.int32, head_weight.shape[1])

    def block_stats(first):
        rows = lax.dynamic_slice_in_dim(normed, first, block, 0)
        wanted = lax.dynamic_slice_in_dim(targets, first, block, 0)
        logits = jnp.dot(rows, head_weight, preferred_element_type=jnp.float32)
        largest = lax.optimization_barrier(jnp.max(logits, axis=1))
        powers = jnp.exp(logits - largest[:, None])
        picked = lax.optimization_barrier(jnp.sum(jnp.where(columns[None, :] == wanted[:, None], logits, 0.0), axis=1))
        return (largest, lax.optimization_barrier(jnp.sum(powers, axis=1)), lax.optimization_barrier(jnp.sum(powers * logits, axis=1)), picked)
    firsts = (lax.iota(jnp.int32, tokens // block) * block).astype(jnp.int32)
    results = lax.map(block_stats, firsts)
    largest, total, weighted, picked = [pieces.reshape(tokens) for pieces in results]
    log_total = jnp.log(total)
    logprob_dealt = picked - largest - log_total
    entropy = largest + log_total - weighted / total
    rms = jnp.sqrt(mean_sq + epsilon)
    token_logprob = jnp.zeros((tokens,), jnp.float32).at[deal].set(logprob_dealt)
    ends = jnp.cumsum(lengths).astype(jnp.int32)
    starts = (ends - lengths).astype(jnp.int32)
    positions = lax.iota(jnp.int32, tokens)
    member = (positions[None, :] >= starts[:, None]) & (positions[None, :] < ends[:, None])
    packed = jnp.zeros((3, tokens), jnp.float32).at[:, deal].set(jnp.stack([logprob_dealt, entropy, rms]))
    peaks = jnp.zeros((tokens,), jnp.float32).at[deal].set(largest)
    sums = lax.optimization_barrier(jnp.sum(jnp.where(member[None], packed[:, None, :], 0.0), axis=2))
    highest = lax.optimization_barrier(jnp.max(jnp.where(member, peaks[None, :], -1e+30), axis=1))
    counts = lengths.astype(jnp.float32)
    request_stats = jnp.concatenate([sums / counts[None, :], highest[None, :]], axis=0)
    return (token_logprob, request_stats)
```

```python
import functools

import jax
import jax.numpy as jnp
from jax import lax
from jax.experimental import pallas as pl
from jax.experimental.pallas import tpu as pltpu
from jax.sharding import PartitionSpec as P

D = 2048
epsilon = 1e-06
LOW = -1e30
TINY = 1e-30
STEPS = 32767.0
DEPTH = 3
LANES = 128
WIDTH = 4


def kernel(
    cfg,
    ints_ref,
    gain_ref,
    hid_ref,
    w_ref,
    tok_ref,
    stat_ref,
    ints_all,
    sq_buf,
    msq_all,
    nrm,
    wbuf,
    sbuf,
    rbuf,
    xbuf,
    ybuf,
    zsend,
    zrecv,
    m_acc,
    t_acc,
    g_acc,
    p_acc,
    st1,
    st2,
    i_send,
    i_recv,
    q_send,
    q_recv,
    h_send,
    h_recv,
    f_send,
    f_recv,
    r_send,
    r_recv,
    wl_sem,
    w_send,
    w_recv,
    y_send,
    y_recv,
    z_send,
    z_recv,
    a_send,
    a_recv,
    b_send,
    b_recv,
):
    V, rows, tokens, feats, slab, quarter, cn, n, mb, reqs = cfg
    v = lax.axis_index("vocab")
    w = lax.axis_index("width")
    lo = lax.rem(w, 2)
    hi = w // 2
    mate = w + 1 - 2 * lo
    far = w + 2 - 4 * hi
    bw = tokens // WIDTH

    def rcopy(src, dst, ss, rs, where):
        return pltpu.make_async_remote_copy(
            src_ref=src,
            dst_ref=dst,
            send_sem=ss,
            recv_sem=rs,
            device_id=where,
            device_id_type=pl.DeviceIdType.MESH,
        )

    def vpeer(d):
        return lax.rem(v + d, V)

    def vsource(d):
        return lax.rem(v + V - d, V)

    def wpeer(d):
        return lax.rem(w + d, WIDTH)

    def wsource(d):
        return lax.rem(w + WIDTH - d, WIDTH)

    def wcols(k, is_keep, dev):
        dev_far = dev + 2 - 4 * (dev // 2)
        q = dev if is_keep else dev_far
        base = k - n if is_keep else k
        return pl.ds(pl.multiple_of(q * quarter + base * cn, LANES), cn)

    own_half = pl.ds(pl.multiple_of(lo * feats, LANES), feats)
    mate_half = pl.ds(pl.multiple_of((1 - lo) * feats, LANES), feats)

    def wlocal(k, is_keep):
        return pltpu.make_async_copy(
            w_ref.at[:, wcols(k, is_keep, w)], wbuf.at[k, own_half, :], wl_sem.at[k]
        )

    def wremote(k, is_keep):
        return rcopy(
            w_ref.at[:, wcols(k, is_keep, mate)],
            wbuf.at[k, own_half, :],
            w_send.at[k],
            w_recv.at[k],
            (v, mate),
        )

    def wstart(k, is_keep):
        wremote(k, is_keep).start()
        wlocal(k, is_keep).start()

    def wwait(k, is_keep):
        wlocal(k, is_keep).wait()
        rcopy(
            w_ref.at[:, wcols(k, is_keep, mate)],
            wbuf.at[k, mate_half, :],
            w_send.at[k],
            w_recv.at[k],
            (v, mate),
        ).wait_recv()

    barrier = pltpu.get_barrier_semaphore()

    @pl.loop(1, WIDTH)
    def _(d):
        pl.semaphore_signal(
            barrier, inc=1, device_id=(v, wpeer(d)), device_id_type=pl.DeviceIdType.MESH
        )

    @pl.loop(1, V)
    def _(d):
        pl.semaphore_signal(
            barrier, inc=1, device_id=(vpeer(d), w), device_id_type=pl.DeviceIdType.MESH
        )

    x = hid_ref[...].astype(jnp.float32)
    sq = jnp.sum(x * x, axis=1, keepdims=True)
    sq_buf[w] = jnp.broadcast_to(sq, (rows, LANES))
    ints_all[pl.ds(pl.multiple_of(w * bw, 8), bw), :] = ints_ref[...]
    pl.semaphore_wait(barrier, WIDTH - 1 + V - 1)

    def qcopy(d, dev):
        return rcopy(sq_buf.at[w], sq_buf.at[dev], q_send.at[d], q_recv.at[d], (v, wpeer(d)))

    def icopy(d, dev):
        span = pl.ds(pl.multiple_of(dev * bw, 8), bw)
        return rcopy(ints_ref, ints_all.at[span, :], i_send.at[d], i_recv.at[d], (v, wpeer(d)))

    @pl.loop(1, WIDTH)
    def _(d):
        qcopy(d, w).start()

    @pl.loop(0, DEPTH)
    def _(k):
        wstart(k, False)

    @pl.loop(1, WIDTH)
    def _(d):
        qcopy(d, wsource(d)).wait_recv()

    total_sq = sq_buf[0] + sq_buf[1] + sq_buf[2] + sq_buf[3]
    mean_sq = total_sq * (1.0 / D)

    def vspan(dev):
        return pl.ds(pl.multiple_of(dev * rows, 16), rows)

    msq_all[vspan(v), :] = mean_sq
    scale = lax.rsqrt(mean_sq[:, 0:1] + epsilon)
    nrm[vspan(v), own_half] = (x * scale * gain_ref[...]).astype(jnp.bfloat16)

    def hcopy(d, dev):
        return rcopy(
            nrm.at[vspan(v), own_half],
            nrm.at[vspan(dev), own_half],
            h_send.at[d],
            h_recv.at[d],
            (vpeer(d), w),
        )

    def fcopy(d, half):
        part = nrm.at[vspan(vsource(d)), half]
        return rcopy(part, part, f_send.at[d], f_recv.at[d], (v, mate))

    def rmscopy(d, dev):
        return rcopy(
            msq_all.at[vspan(v), :],
            msq_all.at[vspan(dev), :],
            r_send.at[d],
            r_recv.at[d],
            (vpeer(d), w),
        )

    @pl.loop(1, V)
    def _(d):
        hcopy(d, v).start()

    fcopy(0, own_half).start()

    @pl.loop(1, V)
    def _(d):
        hcopy(d, vsource(d)).wait_recv()
        fcopy(d, own_half).start()

    @pl.loop(0, n - DEPTH)
    def _(i):
        wstart(n + i, True)
        wstart(DEPTH + i, False)

    @pl.loop(n - DEPTH, n)
    def _(i):
        wstart(n + i, True)

    @pl.loop(1, WIDTH)
    def _(d):
        icopy(d, w).start()

    @pl.loop(1, V)
    def _(d):
        rmscopy(d, v).start()

    m_acc[...] = jnp.full((tokens, LANES), LOW, jnp.float32)
    t_acc[...] = jnp.zeros((tokens, LANES), jnp.float32)
    g_acc[...] = jnp.zeros((tokens, LANES), jnp.float32)
    p_acc[...] = jnp.zeros((tokens, LANES), jnp.float32)

    @pl.loop(0, V)
    def _(d):
        fcopy(d, mate_half).wait_recv()

    def ycopy(i):
        return rcopy(sbuf.at[i], rbuf.at[i], y_send.at[i], y_recv.at[i], (v, far))

    def zcopy(i):
        return rcopy(zsend.at[i], zrecv.at[i], z_send.at[i], z_recv.at[i], (v, far))

    def ystart(i):
        zcopy(i).start()
        ycopy(i).start()

    def yarrive(i):
        zcopy(i).wait_recv()
        ycopy(i).wait_recv()

    def send_dot(i):
        wwait(i, False)

        def multiply(r, peak):
            span = pl.ds(pl.multiple_of(r * mb, 16), mb)
            z = jnp.dot(nrm[span, :], wbuf[i], preferred_element_type=jnp.float32)
            ybuf[span, :] = z
            return jnp.maximum(peak, jnp.max(jnp.abs(z), axis=0, keepdims=True))

        peak = lax.fori_loop(
            0, tokens // mb, multiply, jnp.full((1, cn), TINY, jnp.float32)
        )
        zsend[i] = peak * (1.0 / STEPS)
        rate = STEPS / peak

        @pl.loop(0, tokens // rows)
        def _(r):
            span = pl.ds(pl.multiple_of(r * rows, 16), rows)
            sbuf[i, span, :] = (
                jnp.round(ybuf[span, :] * rate).astype(jnp.int32).astype(jnp.int16)
            )

    def keep_dot(i):
        wwait(n + i, True)

        @pl.loop(0, tokens // mb)
        def _(r):
            span = pl.ds(pl.multiple_of(r * mb, 16), mb)
            xbuf[span, :] = jnp.dot(
                nrm[span, :], wbuf[n + i], preferred_element_type=jnp.float32
            )

    rb = rows
    first_column = v * slab + w * quarter

    def stats(i):
        @pl.loop(0, tokens // rb)
        def _(r):
            span = pl.ds(pl.multiple_of(r * rb, 16), rb)
            target = ints_all[span, 0:1]
            lane = lax.broadcasted_iota(jnp.int32, (rb, LANES), 1)
            aim = jnp.broadcast_to(target, (rb, LANES)) - lane - (first_column + i * cn)
            xs = [
                xbuf[span, g * LANES : (g + 1) * LANES]
                + rbuf[i, span, g * LANES : (g + 1) * LANES].astype(jnp.int32).astype(jnp.float32)
                * zrecv[i, 0:1, g * LANES : (g + 1) * LANES]
                for g in range(cn // LANES)
            ]
            m_old = m_acc[span, :]
            m_new = functools.reduce(jnp.maximum, xs, m_old)
            decay = jnp.exp(m_old - m_new)
            t = t_acc[span, :] * decay
            g_ = g_acc[span, :] * decay
            p = p_acc[span, :]
            for g, z in enumerate(xs):
                e = jnp.exp(z - m_new)
                t = t + e
                g_ = g_ + e * z
                p = p + jnp.where(aim == g * LANES, z, 0.0)
            m_acc[span, :] = m_new
            t_acc[span, :] = t
            g_acc[span, :] = g_
            p_acc[span, :] = p

    @pl.loop(0, DEPTH)
    def _(i):
        send_dot(i)
        ystart(i)

    @pl.loop(1, WIDTH)
    def _(d):
        icopy(d, wsource(d)).wait_recv()

    @pl.loop(0, n - DEPTH)
    def _(i):
        keep_dot(i)
        send_dot(i + DEPTH)
        yarrive(i)
        ystart(i + DEPTH)
        stats(i)

    @pl.loop(n - DEPTH, n)
    def _(i):
        keep_dot(i)
        yarrive(i)
        stats(i)

    m = m_acc[...]
    top = jnp.max(m, axis=1, keepdims=True)
    share = jnp.exp(m - top)
    tot = jnp.sum(t_acc[...] * share, axis=1, keepdims=True)
    wei = jnp.sum(g_acc[...] * share, axis=1, keepdims=True)
    pic = jnp.sum(p_acc[...], axis=1, keepdims=True)
    lane = lax.broadcasted_iota(jnp.int32, (tokens, LANES), 1)
    table = jnp.where(
        lane == 0, top, jnp.where(lane == 1, tot, jnp.where(lane == 2, wei, pic))
    )
    st1[w] = jnp.transpose(table)[0:8, :]

    def acopy(d, dev):
        return rcopy(st1.at[w], st1.at[dev], a_send.at[d], a_recv.at[d], (v, wpeer(d)))

    def bcopy(d, dev):
        return rcopy(st2.at[v], st2.at[dev], b_send.at[d], b_recv.at[d], (vpeer(d), w))

    def joined(parts):
        top = functools.reduce(jnp.maximum, [s[0:1, :] for s in parts])
        tot = jnp.zeros_like(top)
        wei = jnp.zeros_like(top)
        pic = jnp.zeros_like(top)
        for s in parts:
            share = jnp.exp(s[0:1, :] - top)
            tot = tot + s[1:2, :] * share
            wei = wei + s[2:3, :] * share
            pic = pic + s[3:4, :]
        return top, tot, wei, pic

    @pl.loop(1, WIDTH)
    def _(d):
        acopy(d, w).start()

    @pl.loop(1, WIDTH)
    def _(d):
        acopy(d, wsource(d)).wait_recv()

    sub = lax.broadcasted_iota(jnp.int32, (8, tokens), 0)
    top, tot, wei, pic = joined([st1[q] for q in range(WIDTH)])
    st2[v] = jnp.where(sub == 0, top, jnp.where(sub == 1, tot, jnp.where(sub == 2, wei, pic)))

    @pl.loop(1, V)
    def _(d):
        bcopy(d, v).start()

    @pl.loop(1, V)
    def _(d):
        rmscopy(d, vsource(d)).wait_recv()

    @pl.loop(1, V)
    def _(d):
        bcopy(d, vsource(d)).wait_recv()

    top, tot, wei, pic = joined([st2[q] for q in range(V)])
    big = lax.broadcasted_iota(jnp.int32, (LANES, tokens), 0)
    table = jnp.transpose(
        jnp.where(big == 0, top, jnp.where(big == 1, tot, jnp.where(big == 2, wei, pic)))
    )
    largest = table[:, 0:1]
    log_total = jnp.log(table[:, 1:2])
    logprob = table[:, 3:4] - largest - log_total
    entropy = largest + log_total - table[:, 2:3] / table[:, 1:2]
    rms = jnp.sqrt(msq_all[:, 0:1] + epsilon)
    deal = ints_all[:, 1:2]

    wide = tok_ref.shape[1]
    spots = lax.broadcasted_iota(jnp.int32, (tokens, wide), 1) + v * rows
    tok_ref[...] = jnp.sum(
        jnp.where(deal == spots, logprob, 0.0), axis=0, keepdims=True
    )

    lens = ints_ref[0:reqs, 2:3].astype(jnp.float32)
    r_row = lax.broadcasted_iota(jnp.int32, (reqs, LANES), 1)
    s_row = lax.broadcasted_iota(jnp.int32, (reqs, LANES), 0)
    ends = jnp.sum(jnp.where(s_row <= r_row, lens, 0.0), axis=0, keepdims=True)
    starts = jnp.sum(jnp.where(s_row < r_row, lens, 0.0), axis=0, keepdims=True)
    counts = ends - starts
    place = deal.astype(jnp.float32)
    member = (place >= starts) & (place < ends)
    for row, figure in enumerate((logprob, entropy, rms)):
        summed = jnp.sum(jnp.where(member, figure, 0.0), axis=0, keepdims=True)
        stat_ref[row : row + 1, :] = (summed / counts)[:, 0:reqs]
    highest = jnp.max(jnp.where(member, largest, LOW), axis=0, keepdims=True)
    stat_ref[3:4, :] = highest[:, 0:reqs]

    @pl.loop(1, WIDTH)
    def _(d):
        qcopy(d, w).wait_send()
        icopy(d, w).wait_send()
        acopy(d, w).wait_send()

    fcopy(0, own_half).wait_send()

    @pl.loop(1, V)
    def _(d):
        hcopy(d, v).wait_send()
        fcopy(d, own_half).wait_send()
        rmscopy(d, v).wait_send()
        bcopy(d, v).wait_send()

    @pl.loop(0, n)
    def _(i):
        wremote(i, False).wait_send()
        wremote(n + i, True).wait_send()
        ycopy(i).wait_send()
        zcopy(i).wait_send()


def body(hidden, norm_gain, head_weight, lengths, deal, targets):
    rows, feats = hidden.shape
    V = lax.axis_size("vocab")
    w = lax.axis_index("width")
    tokens = rows * V
    slab = head_weight.shape[1]
    quarter = slab // WIDTH
    cn = next(c for c in (512, 256, 128) if quarter % c == 0)
    n = quarter // cn
    mb = next(c for c in (384, 256, 192, 128, 64, 48, 16) if tokens % c == 0)
    reqs = lengths.shape[0]
    bw = tokens // WIDTH
    wide = -(-rows // LANES) * LANES

    lane = lax.broadcasted_iota(jnp.int32, (bw, LANES), 1)
    padded = jnp.pad(lengths, (0, bw - reqs))
    ints = jnp.where(
        lane == 0, targets[:, None], jnp.where(lane == 1, deal[:, None], padded[:, None])
    )
    chip_gain = lax.dynamic_slice_in_dim(norm_gain, w * feats, feats)
    gain = chip_gain.astype(jnp.float32)[None, :]

    cfg = (V, rows, tokens, feats, slab, quarter, cn, n, mb, reqs)
    f32, bf16 = jnp.float32, jnp.bfloat16
    dma = pltpu.SemaphoreType.DMA
    vmem = pl.BlockSpec(memory_space=pltpu.VMEM)
    tok, stat = pl.pallas_call(
        functools.partial(kernel, cfg),
        out_shape=(
            jax.ShapeDtypeStruct((1, wide), f32),
            jax.ShapeDtypeStruct((4, reqs), f32),
        ),
        in_specs=[vmem, vmem, vmem, pl.BlockSpec(memory_space=pl.ANY)],
        out_specs=(vmem, vmem),
        scratch_shapes=[
            pltpu.VMEM((tokens, LANES), jnp.int32),
            pltpu.VMEM((WIDTH, rows, LANES), f32),
            pltpu.VMEM((tokens, LANES), f32),
            pltpu.VMEM((tokens, 2 * feats), bf16),
            pltpu.VMEM((2 * n, 2 * feats, cn), bf16),
            pltpu.VMEM((n, tokens, cn), jnp.int16),
            pltpu.VMEM((n, tokens, cn), jnp.int16),
            pltpu.VMEM((tokens, cn), f32),
            pltpu.VMEM((tokens, cn), f32),
            pltpu.VMEM((n, 1, cn), f32),
            pltpu.VMEM((n, 1, cn), f32),
            pltpu.VMEM((tokens, LANES), f32),
            pltpu.VMEM((tokens, LANES), f32),
            pltpu.VMEM((tokens, LANES), f32),
            pltpu.VMEM((tokens, LANES), f32),
            pltpu.VMEM((WIDTH, 8, tokens), f32),
            pltpu.VMEM((V, 8, tokens), f32),
            dma((WIDTH,)),
            dma((WIDTH,)),
            dma((WIDTH,)),
            dma((WIDTH,)),
            dma((V,)),
            dma((V,)),
            dma((V,)),
            dma((V,)),
            dma((V,)),
            dma((V,)),
            dma((2 * n,)),
            dma((2 * n,)),
            dma((2 * n,)),
            dma((n,)),
            dma((n,)),
            dma((n,)),
            dma((n,)),
            dma((WIDTH,)),
            dma((WIDTH,)),
            dma((V,)),
            dma((V,)),
        ],
        compiler_params=pltpu.CompilerParams(
            collective_id=0, has_side_effects=True, vmem_limit_bytes=58 << 20
        ),
    )(ints, gain, hidden, head_weight)
    return tok[0, :rows], stat


def solution(mesh):
    return jax.shard_map(
        body,
        mesh=mesh,
        in_specs=(P("vocab", "width"), P(), P("width", "vocab"), P(), P("width"), P("width")),
        out_specs=(P("vocab"), P()),
        check_vma=False,
    )
```

```python
import functools

import jax
import jax.numpy as jnp
from jax import lax
from jax.experimental import pallas as pl
from jax.experimental.pallas import tpu as pltpu
from jax.sharding import PartitionSpec as P

D = 2048
epsilon = 1e-06
LOW = -1e30
TINY = 1e-30
STEPS = 32767.0
DEPTH = 3
LANES = 128
WIDTH = 4


def kernel(
    cfg,
    aim_ref,
    deal_ref,
    lens_ref,
    gain_ref,
    hid_ref,
    w_ref,
    tok_ref,
    stat_ref,
    ints_ref,
    gains,
    ints_all,
    sq_buf,
    msq_all,
    nrm,
    wbuf,
    sbuf,
    rbuf,
    xbuf,
    ybuf,
    zsend,
    zrecv,
    m_acc,
    t_acc,
    g_acc,
    p_acc,
    st1,
    st2,
    i_send,
    i_recv,
    q_send,
    q_recv,
    h_send,
    h_recv,
    f_send,
    f_recv,
    r_send,
    r_recv,
    wl_sem,
    w_send,
    w_recv,
    y_send,
    y_recv,
    z_send,
    z_recv,
    ya_send,
    ya_recv,
    a_send,
    a_recv,
    b_send,
    b_recv,
):
    V, rows, tokens, feats, slab, quarter, cn, n, mb, mb_late, reqs = cfg
    v = lax.axis_index("vocab")
    w = lax.axis_index("width")
    lo = lax.rem(w, 2)
    hi = w // 2
    mate = w + 1 - 2 * lo
    far = w + 2 - 4 * hi
    bw = tokens // WIDTH

    def rcopy(src, dst, ss, rs, where):
        return pltpu.make_async_remote_copy(
            src_ref=src,
            dst_ref=dst,
            send_sem=ss,
            recv_sem=rs,
            device_id=where,
            device_id_type=pl.DeviceIdType.MESH,
        )

    def vpeer(d):
        return lax.rem(v + d, V)

    def vsource(d):
        return lax.rem(v + V - d, V)

    def wpeer(d):
        return lax.rem(w + d, WIDTH)

    def wsource(d):
        return lax.rem(w + WIDTH - d, WIDTH)

    def wcols(k, is_keep, dev):
        dev_far = dev + 2 - 4 * (dev // 2)
        q = dev if is_keep else dev_far
        base = k - n if is_keep else k
        return pl.ds(pl.multiple_of(q * quarter + base * cn, LANES), cn)

    own_half = pl.ds(pl.multiple_of(lo * feats, LANES), feats)
    mate_half = pl.ds(pl.multiple_of((1 - lo) * feats, LANES), feats)

    def wlocal(k, is_keep):
        return pltpu.make_async_copy(
            w_ref.at[:, wcols(k, is_keep, w)], wbuf.at[k, own_half, :], wl_sem.at[k]
        )

    def wremote(k, is_keep):
        return rcopy(
            w_ref.at[:, wcols(k, is_keep, mate)],
            wbuf.at[k, own_half, :],
            w_send.at[k],
            w_recv.at[k],
            (v, mate),
        )

    def wstart(k, is_keep):
        wremote(k, is_keep).start()
        wlocal(k, is_keep).start()

    def wwait(k, is_keep):
        wlocal(k, is_keep).wait()
        rcopy(
            w_ref.at[:, wcols(k, is_keep, mate)],
            wbuf.at[k, mate_half, :],
            w_send.at[k],
            w_recv.at[k],
            (v, mate),
        ).wait_recv()

    barrier = pltpu.get_barrier_semaphore()

    @pl.loop(1, WIDTH)
    def _(d):
        pl.semaphore_signal(
            barrier, inc=1, device_id=(v, wpeer(d)), device_id_type=pl.DeviceIdType.MESH
        )

    @pl.loop(1, V)
    def _(d):
        pl.semaphore_signal(
            barrier, inc=1, device_id=(vpeer(d), w), device_id_type=pl.DeviceIdType.MESH
        )

    x = hid_ref[...].astype(jnp.float32)
    sq = jnp.sum(x * x, axis=1, keepdims=True)
    sq_buf[w] = jnp.broadcast_to(sq, (rows, LANES))
    gains[...] = gain_ref[...].astype(jnp.float32)
    pl.semaphore_wait(barrier, WIDTH - 1 + V - 1)

    def qcopy(d, dev):
        return rcopy(sq_buf.at[w], sq_buf.at[dev], q_send.at[d], q_recv.at[d], (v, wpeer(d)))

    def icopy(d, dev):
        span = pl.ds(pl.multiple_of(dev * bw, 8), bw)
        return rcopy(ints_ref, ints_all.at[span, :], i_send.at[d], i_recv.at[d], (v, wpeer(d)))

    @pl.loop(1, WIDTH)
    def _(d):
        qcopy(d, w).start()

    @pl.loop(0, DEPTH)
    def _(k):
        wstart(k, False)

    @pl.loop(1, WIDTH)
    def _(d):
        qcopy(d, wsource(d)).wait_recv()

    total_sq = sq_buf[0] + sq_buf[1] + sq_buf[2] + sq_buf[3]
    mean_sq = total_sq * (1.0 / D)

    def vspan(dev):
        return pl.ds(pl.multiple_of(dev * rows, 16), rows)

    msq_all[vspan(v), :] = mean_sq
    scale = lax.rsqrt(mean_sq[:, 0:1] + epsilon)
    scaled = x * scale
    groups = feats // LANES
    for g in range(groups):
        column = pl.ds(pl.multiple_of(lo * feats + g * LANES, LANES), LANES)
        nrm[0:rows, column] = (
            scaled[:, g * LANES : (g + 1) * LANES] * gains[pl.ds(w * groups + g, 1), :]
        ).astype(jnp.bfloat16)

    def slot(d):
        return pl.ds(pl.multiple_of(d * rows, 16), rows)

    def hcopy(d):
        return rcopy(
            nrm.at[slot(0), own_half],
            nrm.at[slot(d), own_half],
            h_send.at[d],
            h_recv.at[d],
            (vpeer(d), w),
        )

    def fcopy(d, half):
        part = nrm.at[slot(d), half]
        return rcopy(part, part, f_send.at[d], f_recv.at[d], (v, mate))

    def rmscopy(d, dev):
        return rcopy(
            msq_all.at[vspan(v), :],
            msq_all.at[vspan(dev), :],
            r_send.at[d],
            r_recv.at[d],
            (vpeer(d), w),
        )

    fcopy(0, own_half).start()

    @pl.loop(1, V)
    def _(d):
        hcopy(d).start()

    @pl.loop(DEPTH, n)
    def _(k):
        wstart(k, False)

    pick_lane = lax.broadcasted_iota(jnp.int32, (1, LANES), 1)

    @pl.loop(0, bw)
    def _(r):
        ints_ref[pl.ds(r, 1), :] = jnp.where(pick_lane == 0, aim_ref[r], deal_ref[r])

    ints_all[pl.ds(pl.multiple_of(w * bw, 8), bw), :] = ints_ref[...]

    m_acc[...] = jnp.full((tokens, LANES), LOW, jnp.float32)
    t_acc[...] = jnp.zeros((tokens, LANES), jnp.float32)
    g_acc[...] = jnp.zeros((tokens, LANES), jnp.float32)
    p_acc[...] = jnp.zeros((tokens, LANES), jnp.float32)

    late = tokens - rows

    def ycopy(i):
        part = pl.ds(rows, late)
        return rcopy(
            sbuf.at[i, part, :], rbuf.at[i, part, :], y_send.at[i], y_recv.at[i], (v, far)
        )

    def yacopy(i):
        part = pl.ds(0, rows)
        return rcopy(
            sbuf.at[i, part, :], rbuf.at[i, part, :], ya_send.at[i], ya_recv.at[i], (v, far)
        )

    def zcopy(k):
        return rcopy(zsend.at[k], zrecv.at[k], z_send.at[k], z_recv.at[k], (v, far))

    def ystart(i):
        zcopy(n + i).start()
        ycopy(i).start()

    def yarrive(i):
        zcopy(i).wait_recv()
        yacopy(i).wait_recv()
        zcopy(n + i).wait_recv()
        ycopy(i).wait_recv()

    def quantize(i, span, rate):
        sbuf[i, span, :] = (
            jnp.round(ybuf[span, :] * rate).astype(jnp.int32).astype(jnp.int16)
        )

    def first_dot(i):
        wwait(i, False)
        z = jnp.dot(nrm[0:rows, :], wbuf[i], preferred_element_type=jnp.float32)
        ybuf[0:rows, :] = z
        peak = jnp.maximum(TINY, jnp.max(jnp.abs(z), axis=0, keepdims=True))
        zsend[i] = peak * (1.0 / STEPS)
        quantize(i, pl.ds(0, rows), STEPS / peak)
        zcopy(i).start()
        yacopy(i).start()

    def send_dot(i):
        def multiply(r, peak):
            span = pl.ds(pl.multiple_of(rows + r * mb_late, 16), mb_late)
            z = jnp.dot(nrm[span, :], wbuf[i], preferred_element_type=jnp.float32)
            ybuf[span, :] = z
            return jnp.maximum(peak, jnp.max(jnp.abs(z), axis=0, keepdims=True))

        peak = lax.fori_loop(
            0, late // mb_late, multiply, jnp.full((1, cn), TINY, jnp.float32)
        )
        zsend[n + i] = peak * (1.0 / STEPS)
        rate = STEPS / peak

        @pl.loop(1, V)
        def _(r):
            quantize(i, slot(r), rate)

    def keep_dot(i):
        wwait(n + i, True)

        @pl.loop(0, tokens // mb)
        def _(r):
            span = pl.ds(pl.multiple_of(r * mb, 16), mb)
            xbuf[span, :] = jnp.dot(
                nrm[span, :], wbuf[n + i], preferred_element_type=jnp.float32
            )

    rb = rows
    first_column = v * slab + w * quarter

    def stats(i):
        @pl.loop(0, V)
        def _(r):
            held = slot(r)
            span = vspan(vsource(r))
            late_z = n * ((r + V - 1) // V) + i
            target = ints_all[span, 0:1]
            lane = lax.broadcasted_iota(jnp.int32, (rb, LANES), 1)
            aim = jnp.broadcast_to(target, (rb, LANES)) - lane - (first_column + i * cn)
            xs = [
                xbuf[held, g * LANES : (g + 1) * LANES]
                + rbuf[i, held, g * LANES : (g + 1) * LANES].astype(jnp.int32).astype(jnp.float32)
                * zrecv[late_z, 0:1, g * LANES : (g + 1) * LANES]
                for g in range(cn // LANES)
            ]
            m_old = m_acc[span, :]
            m_new = functools.reduce(jnp.maximum, xs, m_old)
            decay = jnp.exp(m_old - m_new)
            t = t_acc[span, :] * decay
            g_ = g_acc[span, :] * decay
            p = p_acc[span, :]
            for g, z in enumerate(xs):
                e = jnp.exp(z - m_new)
                t = t + e
                g_ = g_ + e * z
                p = p + jnp.where(aim == g * LANES, z, 0.0)
            m_acc[span, :] = m_new
            t_acc[span, :] = t
            g_acc[span, :] = g_
            p_acc[span, :] = p

    def relay(d):
        hcopy(d).wait_recv()
        fcopy(d, own_half).start()

    fcopy(0, mate_half).wait_recv()

    @pl.loop(0, DEPTH)
    def _(i):
        first_dot(i)

    turns = min(n - DEPTH, V - 1)

    @pl.loop(0, turns)
    def _(i):
        first_dot(DEPTH + i)
        relay(1 + i)

    @pl.loop(DEPTH + turns, n)
    def _(i):
        first_dot(i)

    @pl.loop(1 + turns, V)
    def _(d):
        relay(d)

    @pl.loop(0, n)
    def _(i):
        wstart(n + i, True)

    @pl.loop(1, V)
    def _(d):
        fcopy(d, mate_half).wait_recv()

    @pl.loop(0, DEPTH)
    def _(i):
        send_dot(i)
        ystart(i)

    @pl.loop(1, WIDTH)
    def _(d):
        icopy(d, w).start()

    @pl.loop(1, V)
    def _(d):
        rmscopy(d, v).start()

    @pl.loop(1, WIDTH)
    def _(d):
        icopy(d, wsource(d)).wait_recv()

    @pl.loop(0, n - DEPTH)
    def _(i):
        keep_dot(i)
        send_dot(i + DEPTH)
        yarrive(i)
        ystart(i + DEPTH)
        stats(i)

    @pl.loop(n - DEPTH, n)
    def _(i):
        keep_dot(i)
        yarrive(i)
        stats(i)

    m = m_acc[...]
    top = jnp.max(m, axis=1, keepdims=True)
    share = jnp.exp(m - top)
    tot = jnp.sum(t_acc[...] * share, axis=1, keepdims=True)
    wei = jnp.sum(g_acc[...] * share, axis=1, keepdims=True)
    pic = jnp.sum(p_acc[...], axis=1, keepdims=True)
    lane = lax.broadcasted_iota(jnp.int32, (tokens, LANES), 1)
    table = jnp.where(
        lane == 0, top, jnp.where(lane == 1, tot, jnp.where(lane == 2, wei, pic))
    )
    st1[w] = jnp.transpose(table)[0:8, :]

    def acopy(d, dev):
        return rcopy(st1.at[w], st1.at[dev], a_send.at[d], a_recv.at[d], (v, wpeer(d)))

    def bcopy(d, dev):
        return rcopy(st2.at[v], st2.at[dev], b_send.at[d], b_recv.at[d], (vpeer(d), w))

    def joined(parts):
        top = functools.reduce(jnp.maximum, [s[0:1, :] for s in parts])
        tot = jnp.zeros_like(top)
        wei = jnp.zeros_like(top)
        pic = jnp.zeros_like(top)
        for s in parts:
            share = jnp.exp(s[0:1, :] - top)
            tot = tot + s[1:2, :] * share
            wei = wei + s[2:3, :] * share
            pic = pic + s[3:4, :]
        return top, tot, wei, pic

    @pl.loop(1, WIDTH)
    def _(d):
        acopy(d, w).start()

    @pl.loop(1, WIDTH)
    def _(d):
        acopy(d, wsource(d)).wait_recv()

    sub = lax.broadcasted_iota(jnp.int32, (8, tokens), 0)
    top, tot, wei, pic = joined([st1[q] for q in range(WIDTH)])
    st2[v] = jnp.where(sub == 0, top, jnp.where(sub == 1, tot, jnp.where(sub == 2, wei, pic)))

    @pl.loop(1, V)
    def _(d):
        bcopy(d, v).start()

    @pl.loop(1, V)
    def _(d):
        rmscopy(d, vsource(d)).wait_recv()

    @pl.loop(1, V)
    def _(d):
        bcopy(d, vsource(d)).wait_recv()

    top, tot, wei, pic = joined([st2[q] for q in range(V)])
    big = lax.broadcasted_iota(jnp.int32, (LANES, tokens), 0)
    table = jnp.transpose(
        jnp.where(big == 0, top, jnp.where(big == 1, tot, jnp.where(big == 2, wei, pic)))
    )
    largest = table[:, 0:1]
    log_total = jnp.log(table[:, 1:2])
    logprob = table[:, 3:4] - largest - log_total
    entropy = largest + log_total - table[:, 2:3] / table[:, 1:2]
    rms = jnp.sqrt(msq_all[:, 0:1] + epsilon)
    deal = ints_all[:, 1:2]

    spots = lax.broadcasted_iota(jnp.int32, (tokens, rows), 1) + v * rows
    tok_ref[...] = jnp.sum(
        jnp.where(deal == spots, logprob, 0.0), axis=0, keepdims=True
    )

    r_row = lax.broadcasted_iota(jnp.int32, (1, LANES), 1)
    ends = jnp.zeros((1, LANES), jnp.int32)
    counts = jnp.ones((1, LANES), jnp.int32)
    for r in range(reqs):
        ends = ends + jnp.where(r_row >= r, lens_ref[r], 0)
        counts = jnp.where(r_row == r, lens_ref[r], counts)
    starts = (ends - counts).astype(jnp.float32)
    ends = ends.astype(jnp.float32)
    counts = counts.astype(jnp.float32)
    place = deal.astype(jnp.float32)
    member = (place >= starts) & (place < ends)
    for row, figure in enumerate((logprob, entropy, rms)):
        summed = jnp.sum(jnp.where(member, figure, 0.0), axis=0, keepdims=True)
        stat_ref[row : row + 1, :] = (summed / counts)[:, 0:reqs]
    highest = jnp.max(jnp.where(member, largest, LOW), axis=0, keepdims=True)
    stat_ref[3:4, :] = highest[:, 0:reqs]

    @pl.loop(1, WIDTH)
    def _(d):
        qcopy(d, w).wait_send()
        icopy(d, w).wait_send()
        acopy(d, w).wait_send()

    fcopy(0, own_half).wait_send()

    @pl.loop(1, V)
    def _(d):
        hcopy(d).wait_send()
        fcopy(d, own_half).wait_send()
        rmscopy(d, v).wait_send()
        bcopy(d, v).wait_send()

    @pl.loop(0, n)
    def _(i):
        wremote(i, False).wait_send()
        wremote(n + i, True).wait_send()
        ycopy(i).wait_send()
        yacopy(i).wait_send()
        zcopy(i).wait_send()
        zcopy(n + i).wait_send()


def body(hidden, norm_gain, head_weight, lengths, deal, targets):
    rows, feats = hidden.shape
    V = lax.axis_size("vocab")
    tokens = rows * V
    slab = head_weight.shape[1]
    quarter = slab // WIDTH
    cn = next(c for c in (512, 256, 128) if quarter % c == 0)
    n = quarter // cn
    mb = next(c for c in (384, 256, 192, 128, 64, 48, 16) if tokens % c == 0)
    reqs = lengths.shape[0]
    bw = tokens // WIDTH

    gain = norm_gain.reshape(-1, LANES)
    late = tokens - rows
    mb_late = next(c for c in (336, 192, 144, 96, 48, 16) if late % c == 0)

    cfg = (V, rows, tokens, feats, slab, quarter, cn, n, mb, mb_late, reqs)
    f32, bf16 = jnp.float32, jnp.bfloat16
    dma = pltpu.SemaphoreType.DMA
    vmem = pl.BlockSpec(memory_space=pltpu.VMEM)
    smem = pl.BlockSpec(memory_space=pltpu.SMEM)
    tok, stat = pl.pallas_call(
        functools.partial(kernel, cfg),
        out_shape=(
            jax.ShapeDtypeStruct((1, rows), f32),
            jax.ShapeDtypeStruct((4, reqs), f32),
        ),
        in_specs=[smem, smem, smem, vmem, vmem, pl.BlockSpec(memory_space=pl.ANY)],
        out_specs=(vmem, vmem),
        scratch_shapes=[
            pltpu.VMEM((bw, LANES), jnp.int32),
            pltpu.VMEM((D // LANES, LANES), f32),
            pltpu.VMEM((tokens, LANES), jnp.int32),
            pltpu.VMEM((WIDTH, rows, LANES), f32),
            pltpu.VMEM((tokens, LANES), f32),
            pltpu.VMEM((tokens, 2 * feats), bf16),
            pltpu.VMEM((2 * n, 2 * feats, cn), bf16),
            pltpu.VMEM((n, tokens, cn), jnp.int16),
            pltpu.VMEM((n, tokens, cn), jnp.int16),
            pltpu.VMEM((tokens, cn), f32),
            pltpu.VMEM((tokens, cn), f32),
            pltpu.VMEM((2 * n, 1, cn), f32),
            pltpu.VMEM((2 * n, 1, cn), f32),
            pltpu.VMEM((tokens, LANES), f32),
            pltpu.VMEM((tokens, LANES), f32),
            pltpu.VMEM((tokens, LANES), f32),
            pltpu.VMEM((tokens, LANES), f32),
            pltpu.VMEM((WIDTH, 8, tokens), f32),
            pltpu.VMEM((V, 8, tokens), f32),
            dma((WIDTH,)),
            dma((WIDTH,)),
            dma((WIDTH,)),
            dma((WIDTH,)),
            dma((V,)),
            dma((V,)),
            dma((V,)),
            dma((V,)),
            dma((V,)),
            dma((V,)),
            dma((2 * n,)),
            dma((2 * n,)),
            dma((2 * n,)),
            dma((n,)),
            dma((n,)),
            dma((2 * n,)),
            dma((2 * n,)),
            dma((n,)),
            dma((n,)),
            dma((WIDTH,)),
            dma((WIDTH,)),
            dma((V,)),
            dma((V,)),
        ],
        compiler_params=pltpu.CompilerParams(
            collective_id=0, has_side_effects=True, vmem_limit_bytes=58 << 20
        ),
    )(targets, deal, lengths, gain, hidden, head_weight)
    return tok[0], stat


def solution(mesh):
    return jax.shard_map(
        body,
        mesh=mesh,
        in_specs=(P("vocab", "width"), P(), P("width", "vocab"), P(), P("width"), P("width")),
        out_specs=(P("vocab"), P()),
        check_vma=False,
    )
```

```python
import functools

import jax
import jax.numpy as jnp
from jax import lax
from jax.experimental import pallas as pl
from jax.experimental.pallas import tpu as pltpu
from jax.sharding import PartitionSpec as P

D = 2048
epsilon = 1e-06
LOW = -1e30
TINY = 1e-30
STEPS = 32767.0
DEPTH = 3
LANES = 128
WIDTH = 4


def kernel(
    cfg,
    aim_ref,
    deal_ref,
    lens_ref,
    gain_ref,
    hid_ref,
    w_ref,
    tok_ref,
    stat_ref,
    ints_ref,
    gains,
    ints_all,
    sq_buf,
    msq_all,
    nrm,
    wbuf,
    sbuf,
    rbuf,
    xbuf,
    ybuf,
    zsend,
    zrecv,
    m_acc,
    t_acc,
    g_acc,
    p_acc,
    st1,
    st2,
    i_send,
    i_recv,
    q_send,
    q_recv,
    h_send,
    h_recv,
    f_send,
    f_recv,
    r_send,
    r_recv,
    wl_sem,
    w_send,
    w_recv,
    y_send,
    y_recv,
    z_send,
    z_recv,
    ya_send,
    ya_recv,
    a_send,
    a_recv,
    b_send,
    b_recv,
):
    V, rows, tokens, feats, slab, quarter, cn, n, mb, mb_late, reqs = cfg
    v = lax.axis_index("vocab")
    w = lax.axis_index("width")
    lo = lax.rem(w, 2)
    hi = w // 2
    mate = w + 1 - 2 * lo
    far = w + 2 - 4 * hi
    bw = tokens // WIDTH

    def rcopy(src, dst, ss, rs, where):
        return pltpu.make_async_remote_copy(
            src_ref=src,
            dst_ref=dst,
            send_sem=ss,
            recv_sem=rs,
            device_id=where,
            device_id_type=pl.DeviceIdType.MESH,
        )

    def vpeer(d):
        return lax.rem(v + d, V)

    def vsource(d):
        return lax.rem(v + V - d, V)

    def wpeer(d):
        return lax.rem(w + d, WIDTH)

    def wsource(d):
        return lax.rem(w + WIDTH - d, WIDTH)

    def wcols(k, is_keep, dev):
        dev_far = dev + 2 - 4 * (dev // 2)
        q = dev if is_keep else dev_far
        base = k - n if is_keep else k
        return pl.ds(pl.multiple_of(q * quarter + base * cn, LANES), cn)

    own_half = pl.ds(pl.multiple_of(lo * feats, LANES), feats)
    mate_half = pl.ds(pl.multiple_of((1 - lo) * feats, LANES), feats)

    def wlocal(k, is_keep):
        return pltpu.make_async_copy(
            w_ref.at[:, wcols(k, is_keep, w)], wbuf.at[k, own_half, :], wl_sem.at[k]
        )

    def wremote(k, is_keep):
        return rcopy(
            w_ref.at[:, wcols(k, is_keep, mate)],
            wbuf.at[k, own_half, :],
            w_send.at[k],
            w_recv.at[k],
            (v, mate),
        )

    def wstart(k, is_keep):
        wremote(k, is_keep).start()
        wlocal(k, is_keep).start()

    def wwait(k, is_keep):
        wlocal(k, is_keep).wait()
        rcopy(
            w_ref.at[:, wcols(k, is_keep, mate)],
            wbuf.at[k, mate_half, :],
            w_send.at[k],
            w_recv.at[k],
            (v, mate),
        ).wait_recv()

    barrier = pltpu.get_barrier_semaphore()

    @pl.loop(1, WIDTH)
    def _(d):
        pl.semaphore_signal(
            barrier, inc=1, device_id=(v, wpeer(d)), device_id_type=pl.DeviceIdType.MESH
        )

    @pl.loop(1, V)
    def _(d):
        pl.semaphore_signal(
            barrier, inc=1, device_id=(vpeer(d), w), device_id_type=pl.DeviceIdType.MESH
        )

    x = hid_ref[...].astype(jnp.float32)
    sq = jnp.sum(x * x, axis=1, keepdims=True)
    sq_buf[w] = jnp.broadcast_to(sq, (rows, LANES))
    gains[...] = gain_ref[...].astype(jnp.float32)
    pl.semaphore_wait(barrier, WIDTH - 1 + V - 1)

    def qcopy(d, dev):
        return rcopy(sq_buf.at[w], sq_buf.at[dev], q_send.at[d], q_recv.at[d], (v, wpeer(d)))

    def icopy(d, dev):
        span = pl.ds(pl.multiple_of(dev * bw, 8), bw)
        return rcopy(ints_ref, ints_all.at[span, :], i_send.at[d], i_recv.at[d], (v, wpeer(d)))

    @pl.loop(1, WIDTH)
    def _(d):
        qcopy(d, w).start()

    @pl.loop(0, DEPTH)
    def _(k):
        wstart(k, False)

    @pl.loop(1, WIDTH)
    def _(d):
        qcopy(d, wsource(d)).wait_recv()

    total_sq = sq_buf[0] + sq_buf[1] + sq_buf[2] + sq_buf[3]
    mean_sq = total_sq * (1.0 / D)

    def vspan(dev):
        return pl.ds(pl.multiple_of(dev * rows, 16), rows)

    msq_all[vspan(v), :] = mean_sq
    scale = lax.rsqrt(mean_sq[:, 0:1] + epsilon)
    scaled = x * scale
    groups = feats // LANES
    for g in range(groups):
        column = pl.ds(pl.multiple_of(lo * feats + g * LANES, LANES), LANES)
        nrm[0:rows, column] = (
            scaled[:, g * LANES : (g + 1) * LANES] * gains[pl.ds(w * groups + g, 1), :]
        ).astype(jnp.bfloat16)

    def slot(d):
        return pl.ds(pl.multiple_of(d * rows, 16), rows)

    def hcopy(d):
        return rcopy(
            nrm.at[slot(0), own_half],
            nrm.at[slot(d), own_half],
            h_send.at[d],
            h_recv.at[d],
            (vpeer(d), w),
        )

    def fcopy(d, half):
        part = nrm.at[slot(d), half]
        return rcopy(part, part, f_send.at[d], f_recv.at[d], (v, mate))

    def rmscopy(d, dev):
        return rcopy(
            msq_all.at[vspan(v), :],
            msq_all.at[vspan(dev), :],
            r_send.at[d],
            r_recv.at[d],
            (vpeer(d), w),
        )

    fcopy(0, own_half).start()

    @pl.loop(1, V)
    def _(d):
        hcopy(d).start()

    @pl.loop(DEPTH, n)
    def _(k):
        wstart(k, False)

    pick_lane = lax.broadcasted_iota(jnp.int32, (1, LANES), 1)

    @pl.loop(0, bw)
    def _(r):
        ints_ref[pl.ds(r, 1), :] = jnp.where(pick_lane == 0, aim_ref[r], deal_ref[r])

    ints_all[pl.ds(pl.multiple_of(w * bw, 8), bw), :] = ints_ref[...]

    m_acc[...] = jnp.full((tokens, LANES), LOW, jnp.float32)
    t_acc[...] = jnp.zeros((tokens, LANES), jnp.float32)
    g_acc[...] = jnp.zeros((tokens, LANES), jnp.float32)
    p_acc[...] = jnp.zeros((tokens, LANES), jnp.float32)

    late = tokens - rows

    def ycopy(i):
        part = pl.ds(rows, late)
        return rcopy(
            sbuf.at[i, part, :], rbuf.at[i, part, :], y_send.at[i], y_recv.at[i], (v, far)
        )

    def yacopy(i):
        part = pl.ds(0, rows)
        return rcopy(
            sbuf.at[i, part, :], rbuf.at[i, part, :], ya_send.at[i], ya_recv.at[i], (v, far)
        )

    def zcopy(k):
        return rcopy(zsend.at[k], zrecv.at[k], z_send.at[k], z_recv.at[k], (v, far))

    def ystart(i):
        zcopy(n + i).start()
        ycopy(i).start()

    def yarrive(i):
        zcopy(i).wait_recv()
        yacopy(i).wait_recv()
        zcopy(n + i).wait_recv()
        ycopy(i).wait_recv()

    def quantize(i, span, rate):
        sbuf[i, span, :] = (
            jnp.round(ybuf[span, :] * rate).astype(jnp.int32).astype(jnp.int16)
        )

    def first_dot(i):
        wwait(i, False)
        z = jnp.dot(nrm[0:rows, :], wbuf[i], preferred_element_type=jnp.float32)
        ybuf[0:rows, :] = z
        peak = jnp.maximum(TINY, jnp.max(jnp.abs(z), axis=0, keepdims=True))
        zsend[i] = peak * (1.0 / STEPS)
        quantize(i, pl.ds(0, rows), STEPS / peak)
        zcopy(i).start()
        yacopy(i).start()

    def send_dot(i):
        def multiply(r, peak):
            span = pl.ds(pl.multiple_of(rows + r * mb_late, 16), mb_late)
            z = jnp.dot(nrm[span, :], wbuf[i], preferred_element_type=jnp.float32)
            ybuf[span, :] = z
            return jnp.maximum(peak, jnp.max(jnp.abs(z), axis=0, keepdims=True))

        peak = lax.fori_loop(
            0, late // mb_late, multiply, jnp.full((1, cn), TINY, jnp.float32)
        )
        zsend[n + i] = peak * (1.0 / STEPS)
        rate = STEPS / peak

        @pl.loop(1, V)
        def _(r):
            quantize(i, slot(r), rate)

    def keep_dot(i):
        wwait(n + i, True)

        @pl.loop(0, tokens // mb)
        def _(r):
            span = pl.ds(pl.multiple_of(r * mb, 16), mb)
            xbuf[span, :] = jnp.dot(
                nrm[span, :], wbuf[n + i], preferred_element_type=jnp.float32
            )

    rb = rows
    first_column = v * slab + w * quarter

    def stats(i):
        @pl.loop(0, V)
        def _(r):
            held = slot(r)
            span = vspan(vsource(r))
            late_z = n * ((r + V - 1) // V) + i
            target = ints_all[span, 0:1]
            lane = lax.broadcasted_iota(jnp.int32, (rb, LANES), 1)
            aim = jnp.broadcast_to(target, (rb, LANES)) - lane - (first_column + i * cn)
            xs = [
                xbuf[held, g * LANES : (g + 1) * LANES]
                + rbuf[i, held, g * LANES : (g + 1) * LANES].astype(jnp.int32).astype(jnp.float32)
                * zrecv[late_z, 0:1, g * LANES : (g + 1) * LANES]
                for g in range(cn // LANES)
            ]
            m_old = m_acc[span, :]
            m_new = functools.reduce(jnp.maximum, xs, m_old)
            decay = jnp.exp(m_old - m_new)
            t = t_acc[span, :] * decay
            g_ = g_acc[span, :] * decay
            p = p_acc[span, :]
            for g, z in enumerate(xs):
                e = jnp.exp(z - m_new)
                t = t + e
                g_ = g_ + e * z
                p = p + jnp.where(aim == g * LANES, z, 0.0)
            m_acc[span, :] = m_new
            t_acc[span, :] = t
            g_acc[span, :] = g_
            p_acc[span, :] = p

    def relay(d):
        hcopy(d).wait_recv()
        fcopy(d, own_half).start()

    fcopy(0, mate_half).wait_recv()

    @pl.loop(0, DEPTH)
    def _(i):
        first_dot(i)

    turns = min(n - DEPTH, V - 1)

    @pl.loop(0, turns)
    def _(i):
        first_dot(DEPTH + i)
        relay(1 + i)

    @pl.loop(DEPTH + turns, n)
    def _(i):
        first_dot(i)

    @pl.loop(1 + turns, V)
    def _(d):
        relay(d)

    @pl.loop(0, n)
    def _(i):
        wstart(n + i, True)

    @pl.loop(1, V)
    def _(d):
        fcopy(d, mate_half).wait_recv()

    @pl.loop(0, DEPTH)
    def _(i):
        send_dot(i)
        ystart(i)

    @pl.loop(1, WIDTH)
    def _(d):
        icopy(d, w).start()

    @pl.loop(1, V)
    def _(d):
        rmscopy(d, v).start()

    @pl.loop(1, WIDTH)
    def _(d):
        icopy(d, wsource(d)).wait_recv()

    @pl.loop(0, n - DEPTH)
    def _(i):
        keep_dot(i)
        send_dot(i + DEPTH)
        yarrive(i)
        ystart(i + DEPTH)
        stats(i)

    @pl.loop(n - DEPTH, n)
    def _(i):
        keep_dot(i)
        yarrive(i)
        stats(i)

    m = m_acc[...]
    top = jnp.max(m, axis=1, keepdims=True)
    share = jnp.exp(m - top)
    tot = jnp.sum(t_acc[...] * share, axis=1, keepdims=True)
    wei = jnp.sum(g_acc[...] * share, axis=1, keepdims=True)
    pic = jnp.sum(p_acc[...], axis=1, keepdims=True)
    lane = lax.broadcasted_iota(jnp.int32, (tokens, LANES), 1)
    table = jnp.where(
        lane == 0, top, jnp.where(lane == 1, tot, jnp.where(lane == 2, wei, pic))
    )
    st1[w] = jnp.transpose(table)[0:4, :]

    def acopy(d, dev):
        return rcopy(st1.at[w], st1.at[dev], a_send.at[d], a_recv.at[d], (v, wpeer(d)))

    def bcopy(d, dev):
        return rcopy(st2.at[v], st2.at[dev], b_send.at[d], b_recv.at[d], (vpeer(d), w))

    def joined(parts):
        top = functools.reduce(jnp.maximum, [s[0:1, :] for s in parts])
        tot = jnp.zeros_like(top)
        wei = jnp.zeros_like(top)
        pic = jnp.zeros_like(top)
        for s in parts:
            share = jnp.exp(s[0:1, :] - top)
            tot = tot + s[1:2, :] * share
            wei = wei + s[2:3, :] * share
            pic = pic + s[3:4, :]
        return top, tot, wei, pic

    @pl.loop(1, WIDTH)
    def _(d):
        acopy(d, w).start()

    @pl.loop(1, WIDTH)
    def _(d):
        acopy(d, wsource(d)).wait_recv()

    sub = lax.broadcasted_iota(jnp.int32, (4, tokens), 0)
    top, tot, wei, pic = joined([st1[q] for q in range(WIDTH)])
    st2[v] = jnp.where(sub == 0, top, jnp.where(sub == 1, tot, jnp.where(sub == 2, wei, pic)))

    @pl.loop(1, V)
    def _(d):
        bcopy(d, v).start()

    @pl.loop(1, V)
    def _(d):
        rmscopy(d, vsource(d)).wait_recv()

    @pl.loop(1, V)
    def _(d):
        bcopy(d, vsource(d)).wait_recv()

    top, tot, wei, pic = joined([st2[q] for q in range(V)])
    big = lax.broadcasted_iota(jnp.int32, (LANES, tokens), 0)
    table = jnp.transpose(
        jnp.where(big == 0, top, jnp.where(big == 1, tot, jnp.where(big == 2, wei, pic)))
    )
    largest = table[:, 0:1]
    log_total = jnp.log(table[:, 1:2])
    logprob = table[:, 3:4] - largest - log_total
    entropy = largest + log_total - table[:, 2:3] / table[:, 1:2]
    rms = jnp.sqrt(msq_all[:, 0:1] + epsilon)
    deal = ints_all[:, 1:2]

    spots = lax.broadcasted_iota(jnp.int32, (tokens, rows), 1) + v * rows
    tok_ref[...] = jnp.sum(
        jnp.where(deal == spots, logprob, 0.0), axis=0, keepdims=True
    )

    r_row = lax.broadcasted_iota(jnp.int32, (1, LANES), 1)
    ends = jnp.zeros((1, LANES), jnp.int32)
    counts = jnp.ones((1, LANES), jnp.int32)
    for r in range(reqs):
        ends = ends + jnp.where(r_row >= r, lens_ref[r], 0)
        counts = jnp.where(r_row == r, lens_ref[r], counts)
    starts = (ends - counts).astype(jnp.float32)
    ends = ends.astype(jnp.float32)
    counts = counts.astype(jnp.float32)
    place = deal.astype(jnp.float32)
    member = (place >= starts) & (place < ends)
    for row, figure in enumerate((logprob, entropy, rms)):
        summed = jnp.sum(jnp.where(member, figure, 0.0), axis=0, keepdims=True)
        stat_ref[row : row + 1, :] = (summed / counts)[:, 0:reqs]
    highest = jnp.max(jnp.where(member, largest, LOW), axis=0, keepdims=True)
    stat_ref[3:4, :] = highest[:, 0:reqs]

    @pl.loop(1, WIDTH)
    def _(d):
        qcopy(d, w).wait_send()
        icopy(d, w).wait_send()
        acopy(d, w).wait_send()

    fcopy(0, own_half).wait_send()

    @pl.loop(1, V)
    def _(d):
        hcopy(d).wait_send()
        fcopy(d, own_half).wait_send()
        rmscopy(d, v).wait_send()
        bcopy(d, v).wait_send()

    @pl.loop(0, n)
    def _(i):
        wremote(i, False).wait_send()
        wremote(n + i, True).wait_send()
        ycopy(i).wait_send()
        yacopy(i).wait_send()
        zcopy(i).wait_send()
        zcopy(n + i).wait_send()


def body(hidden, norm_gain, head_weight, lengths, deal, targets):
    rows, feats = hidden.shape
    V = lax.axis_size("vocab")
    tokens = rows * V
    slab = head_weight.shape[1]
    quarter = slab // WIDTH
    cn = next(c for c in (512, 256, 128) if quarter % c == 0)
    n = quarter // cn
    mb = next(c for c in (384, 256, 192, 128, 64, 48, 16) if tokens % c == 0)
    reqs = lengths.shape[0]
    bw = tokens // WIDTH

    gain = norm_gain.reshape(-1, LANES)
    late = tokens - rows
    mb_late = next(c for c in (336, 192, 144, 96, 48, 16) if late % c == 0)

    cfg = (V, rows, tokens, feats, slab, quarter, cn, n, mb, mb_late, reqs)
    f32, bf16 = jnp.float32, jnp.bfloat16
    dma = pltpu.SemaphoreType.DMA
    vmem = pl.BlockSpec(memory_space=pltpu.VMEM)
    smem = pl.BlockSpec(memory_space=pltpu.SMEM)
    tok, stat = pl.pallas_call(
        functools.partial(kernel, cfg),
        out_shape=(
            jax.ShapeDtypeStruct((1, rows), f32),
            jax.ShapeDtypeStruct((4, reqs), f32),
        ),
        in_specs=[smem, smem, smem, vmem, vmem, pl.BlockSpec(memory_space=pl.ANY)],
        out_specs=(vmem, vmem),
        scratch_shapes=[
            pltpu.VMEM((bw, LANES), jnp.int32),
            pltpu.VMEM((D // LANES, LANES), f32),
            pltpu.VMEM((tokens, LANES), jnp.int32),
            pltpu.VMEM((WIDTH, rows, LANES), f32),
            pltpu.VMEM((tokens, LANES), f32),
            pltpu.VMEM((tokens, 2 * feats), bf16),
            pltpu.VMEM((2 * n, 2 * feats, cn), bf16),
            pltpu.VMEM((n, tokens, cn), jnp.int16),
            pltpu.VMEM((n, tokens, cn), jnp.int16),
            pltpu.VMEM((tokens, cn), f32),
            pltpu.VMEM((tokens, cn), f32),
            pltpu.VMEM((2 * n, 1, cn), f32),
            pltpu.VMEM((2 * n, 1, cn), f32),
            pltpu.VMEM((tokens, LANES), f32),
            pltpu.VMEM((tokens, LANES), f32),
            pltpu.VMEM((tokens, LANES), f32),
            pltpu.VMEM((tokens, LANES), f32),
            pltpu.VMEM((WIDTH, 4, tokens), f32),
            pltpu.VMEM((V, 4, tokens), f32),
            dma((WIDTH,)),
            dma((WIDTH,)),
            dma((WIDTH,)),
            dma((WIDTH,)),
            dma((V,)),
            dma((V,)),
            dma((V,)),
            dma((V,)),
            dma((V,)),
            dma((V,)),
            dma((2 * n,)),
            dma((2 * n,)),
            dma((2 * n,)),
            dma((n,)),
            dma((n,)),
            dma((2 * n,)),
            dma((2 * n,)),
            dma((n,)),
            dma((n,)),
            dma((WIDTH,)),
            dma((WIDTH,)),
            dma((V,)),
            dma((V,)),
        ],
        compiler_params=pltpu.CompilerParams(
            collective_id=0, has_side_effects=True, vmem_limit_bytes=58 << 20
        ),
    )(targets, deal, lengths, gain, hidden, head_weight)
    return tok[0], stat


def solution(mesh):
    return jax.shard_map(
        body,
        mesh=mesh,
        in_specs=(P("vocab", "width"), P(), P("width", "vocab"), P(), P("width"), P("width")),
        out_specs=(P("vocab"), P()),
        check_vma=False,
    )
```
